32 devices in a mesh: groups: 2 (over y), row: 4 (over z), col: 4 (over x, core).
Axes of the slice: x: 2, y: 2, z: 4, core: 2. Of those that a mesh axis runs over, the one named last changes fastest.
Arguments:
- factor_blocks: bfloat16 [20, 4096, 4096], P('groups', 'row', 'col'), parts along dimension 0, may hold values from -0.0390625 to 0.0390625
- inverse_blocks: bfloat16 [10, 4096, 4096], P('groups', 'col', 'row'), parts along dimension 0, as said below
- right_sides: bfloat16 [10, 4096, 256], P('groups', 'row'), parts along dimension 0, may hold values from -6 to 6
Outputs:
- solution: bfloat16 [10, 4096, 256], P('groups', 'col', 'row'), parts along dimension 0
The draws below stay inside these ranges and needn't reach their ends.
There are 2 independent parts, one for each index of `groups`. The reference program is written for one: setup_inputs(seed, part) draws one part's arguments, and reference() takes and returns one part's arrays. A program takes and returns all parts, laid end to end along the dimension named above; each array names one. Nothing has to cross between parts.
Inputs may be any that keep to these rules, and one draw needn't show every extreme that they name: `inverse_blocks`: each block is lower triangular with a diagonal of 0.5 to 2, hence invertible.
All inputs are finite; a program needn't handle non-finite values.
Results may differ from the reference program's by a relative error of at most 0.0095.
Values may be sent and summed in bfloat16 or wider, within the bound.
A program may use at most 64 MiB of HBM per device.

```python
import jax
import jax.numpy as jnp
from jax import lax

BS = 4096
NB = 5
R = 256
ORDER = 20480
NPAIR = 10
N_ROW = 4


def draw_inverse_blocks(key, part):
    base = jax.random.fold_in(key, 4177)
    key_diag, key_off = jax.random.split(base, 2)
    diagonal = jnp.exp(jax.random.uniform(key_diag, (NB, BS), jnp.float32, jnp.log(0.5), jnp.log(2.0)))
    lower = jax.random.normal(key_off, (NB, BS, BS), jnp.float32) * (0.6 / jnp.sqrt(BS * 1.0))
    rows = jnp.arange(BS)[:, None]
    cols = jnp.arange(BS)[None, :]
    strict = (rows > cols).astype(jnp.float32)
    eye = (rows == cols).astype(jnp.float32)
    whole = diagonal[:, :, None] * eye[None] + lower * strict[None]
    return whole.astype(jnp.bfloat16)


def block_levels(stream_key, extent, shards, smallest, largest):
    def one(position, parts):
        draws = jax.random.uniform(jax.random.fold_in(jax.random.fold_in(stream_key, 6), position), (parts,), jnp.float32, smallest / len(shards), largest / len(shards))
        return jnp.repeat(jnp.exp(draws), extent[position] // parts).reshape((-1,) + (1,) * (len(extent) - position - 1))

    level = one(*shards[0])
    for cut in shards[1:]:
        level = level * one(*cut)
    return level


def normal_values(rng, dims, scale, reach, cuts=(), kind=jnp.bfloat16):
    result = jax.random.normal(rng, dims, jnp.float32) * scale
    if len(cuts) > 0:
        result = block_levels(rng, dims, cuts, -0.22, 0.18) * result
    return jnp.clip(result, min=-reach, max=reach).astype(kind)


def setup_inputs(seed: int = 0, part: int = 0) -> dict:
    seeds = jax.random.split(jax.random.key(seed), 4)
    part_splits = jax.random.split(jax.random.fold_in(seeds[3], part), 4)
    return {
        "factor_blocks": normal_values(part_splits[0], (NPAIR, BS, BS), ORDER ** -0.5, 0.0390625, ((1, 4), (2, 4))),
        "inverse_blocks": draw_inverse_blocks(jax.random.fold_in(jax.random.fold_in(seeds[3], part), 71), part),
        "right_sides": normal_values(part_splits[2], (NB, BS, R), 1.0, 6.0, ((1, 4),)),
    }


def pair_index(block_row, column_index):
    return block_row * (block_row - 1) // 2 + column_index


def reference(factor_blocks, inverse_blocks, right_sides):
    solved = []
    group_rows = BS // N_ROW
    for block_row in range(NB):
        residual = right_sides[block_row].astype(jnp.float32)
        if block_row > 0:
            strip = jnp.concatenate([factor_blocks[pair_index(block_row, j)] for j in range(block_row)], axis=1)
            known = jnp.concatenate(solved, axis=0)
            residual = residual - jnp.dot(strip, known, preferred_element_type=jnp.float32)
        residual_bf = residual.astype(jnp.bfloat16)
        inverse = inverse_blocks[block_row].astype(jnp.float32).reshape(BS, N_ROW, group_rows)
        grouped = residual_bf.astype(jnp.float32).reshape(N_ROW, group_rows, R)
        terms = jnp.einsum("iqk,qkr->qir", inverse, grouped, precision=lax.Precision.HIGHEST)
        solved.append(jnp.sum(terms, axis=0).astype(jnp.bfloat16))
    return jnp.stack(solved, axis=0)
```

```python
import jax
import jax.numpy as jnp
from jax import lax
from jax.experimental import pallas as pl
from jax.experimental.pallas import tpu as pltpu
from jax.sharding import PartitionSpec as P

MESH = pl.DeviceIdType.MESH
CHAINS = 2
PIECES = 4
INVERSE_SLOTS = 3
f32, bf16 = jnp.float32, jnp.bfloat16


def pair_index(block_row, column_index):
    return block_row * (block_row - 1) // 2 + column_index


def dot_t(a, b):
    return lax.dot_general(a, b, (((1,), (1,)), ((), ())), preferred_element_type=f32)


def kernel(
    factor_hbm, inverse_hbm, right_hbm, solved,
    factor, inverse, right, turned, x, in_right, in_left, out, term, partial, ahead, far_out, far_in, residual,
    load_sem, push_send, push_recv, far_send, far_recv, line_send, line_recv, give_send, give_recv, credit,
):
    steps, _, width, piece = solved.shape
    pairs = factor_hbm.shape[0]
    rows = right.shape[1]
    factor_slots = factor.shape[0]
    row = lax.axis_index("row")
    col = lax.axis_index("col")
    group = lax.axis_index("groups")
    core = lax.rem(col, 2)
    side = col // 2
    sibling = (group, row, col + 1 - 2 * core)
    far = (group, row, lax.rem(col + 2, 4))
    left = (group, jnp.maximum(row - 1, 0), col)
    right_dev = (group, jnp.minimum(row + 1, 3), col)
    last = steps - 1

    def remote(src, dst, send, recv, peer):
        return pltpu.make_async_remote_copy(
            src_ref=src, dst_ref=dst, send_sem=send, recv_sem=recv, device_id=peer, device_id_type=MESH
        )

    def local_tile(kind, at):
        if kind == "f":
            return pltpu.make_async_copy(factor_hbm.at[at], factor.at[at % factor_slots, core], load_sem.at[at])
        return pltpu.make_async_copy(inverse_hbm.at[at], inverse.at[at % INVERSE_SLOTS, core], load_sem.at[pairs + at])

    def pushed_tile(kind, at):
        if kind == "f":
            dst = factor.at[at % factor_slots, core]
            return remote(factor_hbm.at[at], dst, push_send.at[at], push_recv.at[at], sibling)
        dst = inverse.at[at % INVERSE_SLOTS, core]
        return remote(inverse_hbm.at[at], dst, push_send.at[pairs + at], push_recv.at[pairs + at], sibling)

    def landed_tile(kind, at):
        if kind == "f":
            dst = factor.at[at % factor_slots, 1 - core]
            return remote(factor_hbm.at[at], dst, push_send.at[at], push_recv.at[at], sibling)
        dst = inverse.at[at % INVERSE_SLOTS, 1 - core]
        return remote(inverse_hbm.at[at], dst, push_send.at[pairs + at], push_recv.at[pairs + at], sibling)

    tiles = [("i", 0)]
    for i in range(1, steps):
        tiles += [("f", pair_index(i, j)) for j in range(i)] + [("i", i)]
    fresh = [t for t in tiles if not (t[0] == "f" and t[1] >= factor_slots or t[0] == "i" and t[1] >= INVERSE_SLOTS)]
    early = [t for t in fresh if t[0] == "i" or t[1] < pair_index(4, 0)]
    late = [t for t in fresh if t not in early]
    ready = set()

    def loaded(kind, at):
        if (kind, at) not in ready:
            ready.add((kind, at))
            local_tile(kind, at).wait()
            landed_tile(kind, at).wait_recv()

    lanes = pl.ds(pl.multiple_of(core * CHAINS * width, CHAINS * width), CHAINS * width)

    def right_load(i):
        return pltpu.make_async_copy(right_hbm.at[i, :, lanes], right.at[i], load_sem.at[pairs + steps + i])

    right_load(0).start()
    for kind, at in fresh[:1]:
        local_tile(kind, at).start()
    for i in range(1, steps):
        right_load(i).start()
    for kind, at in fresh[1:]:
        local_tile(kind, at).start()

    barrier = pltpu.get_barrier_semaphore()
    for peer in (sibling, far):
        pl.semaphore_signal(barrier, inc=1, device_id=peer, device_id_type=MESH)

    @pl.when(row > 0)
    def _():
        pl.semaphore_signal(barrier, inc=1, device_id=left, device_id_type=MESH)

    @pl.when(row < 3)
    def _():
        pl.semaphore_signal(barrier, inc=1, device_id=right_dev, device_id_type=MESH)

    @pl.when(jnp.logical_or(row == 0, row == 3))
    def _():
        pl.semaphore_wait(barrier, 3)

    @pl.when(jnp.logical_and(row > 0, row < 3))
    def _():
        pl.semaphore_wait(barrier, 4)

    for kind, at in early:
        pushed_tile(kind, at).start()

    def turn(i):
        right_load(i).wait()
        turned[i] = right[i].T

    def going_right(i, k, p, src, dst):
        return remote(src, dst, line_send.at[i, k, 0, p], line_recv.at[i, k, 0, p], right_dev)

    def going_left(i, k, p, src, dst):
        return remote(src, dst, line_send.at[i, k, 1, p], line_recv.at[i, k, 1, p], left)

    def each(body, start=0):
        def step(p, carry):
            body(p, 2 * side + p // 2)
            return carry

        lax.fori_loop(start, PIECES, step, 0)

    def span(p):
        return pl.ds(pl.multiple_of(lax.rem(p, 2) * piece, piece), piece)

    def solve(i, k):
        chain = slice(k * width, (k + 1) * width)
        if i == 0:
            residual[k] = turned[0, chain, :]
        else:
            for h in range(2):
                cols = slice(h * (rows // 2), (h + 1) * (rows // 2))
                far_copy(i, k, h).wait_recv()
                total = partial[k, :, cols] + far_in[i - 1, k, h].astype(f32)
                residual[k, :, cols] = (turned[i, chain, cols].astype(f32) - total).astype(bf16)
        loaded("i", i)
        par = i % 2
        goal = 2 * core + k

        def body(p, c):
            @pl.when(c >= row)
            def _():
                value = dot_t(residual[k], inverse[i % INVERSE_SLOTS, p // 2, span(p), :])
                term[k, p] = value
                out[par, k, p] = value.astype(bf16)
                if i < last:
                    @pl.when(jnp.logical_and(row == 0, c == 0))
                    def _():
                        x[i, k, p] = value.astype(bf16)
                        going_right(i, k, p, x.at[i, k, p], x.at[i, k, p]).start()

                    @pl.when(jnp.logical_and(row == 0, c > 0))
                    def _():
                        going_right(i, k, p, out.at[par, k, p], in_right.at[par, k, p]).start()

                    @pl.when(jnp.logical_and(row >= 2, c == row))
                    def _():
                        going_left(i, k, p, out.at[par, k, p], in_left.at[par, k, p]).start()
                else:
                    @pl.when(jnp.logical_and(row == 0, goal > 0))
                    def _():
                        going_right(i, k, p, out.at[par, k, p], in_right.at[par, k, p]).start()

                    @pl.when(jnp.logical_and(row > goal, c == row))
                    def _():
                        going_left(i, k, p, out.at[par, k, p], in_left.at[par, k, p]).start()

        each(body)

    def came_right(i, k, p):
        going_right(i, k, p, out.at[0, k, p], in_right.at[0, k, p]).wait_recv()

    def came_left(i, k, p):
        going_left(i, k, p, out.at[0, k, p], in_left.at[0, k, p]).wait_recv()

    def relay_first(i, k):
        par = i % 2

        @pl.when(row == 1)
        def _():
            def body(p, c):
                came_right(i, k, p)

                @pl.when(c == 0)
                def _():
                    going_right(i, k, p, x.at[i, k, p], x.at[i, k, p]).start()

                @pl.when(c == 1)
                def _():
                    x[i, k, p] = (in_right[par, k, p].astype(f32) + term[k, p]).astype(bf16)
                    going_right(i, k, p, x.at[i, k, p], x.at[i, k, p]).start()
                    going_left(i, k, p, x.at[i, k, p], x.at[i, k, p]).start()

                @pl.when(c >= 2)
                def _():
                    out[par, k, p] = (in_right[par, k, p].astype(f32) + term[k, p]).astype(bf16)
                    going_right(i, k, p, out.at[par, k, p], in_right.at[par, k, p]).start()

            each(body)

        @pl.when(jnp.logical_and(row == 2, side == 1))
        def _():
            def body(p, c):
                came_left(i, k, p)
                out[par, k, p] = (in_left[par, k, p].astype(f32) + term[k, p]).astype(bf16)
                going_left(i, k, p, out.at[par, k, p], in_left.at[par, k, p]).start()

            each(body, PIECES // 2)

    def relay_second(i, k):
        par = i % 2

        @pl.when(jnp.logical_and(row == 1, side == 1))
        def _():
            def body(p, c):
                came_left(i, k, p)
                x[i, k, p] = (out[par, k, p].astype(f32) + in_left[par, k, p].astype(f32)).astype(bf16)
                going_left(i, k, p, x.at[i, k, p], x.at[i, k, p]).start()

            each(body)

        @pl.when(row == 2)
        def _():
            def body(p, c):
                came_right(i, k, p)

                @pl.when(c >= 2)
                def _():
                    x[i, k, p] = (out[par, k, p].astype(f32) + in_right[par, k, p].astype(f32)).astype(bf16)

                going_right(i, k, p, x.at[i, k, p], x.at[i, k, p]).start()

            each(body)

    def came_last(i, k, p, c):
        @pl.when(jnp.logical_and(row == 0, c >= 1))
        def _():
            came_left(i, k, p)

        @pl.when(row == 3)
        def _():
            came_right(i, k, p)

    def sent(i, k):
        goal = 2 * core + k
        to_right = row < 3 if i < last else row < goal
        to_left = row > 0 if i < last else row > goal

        def body(p, c):
            @pl.when(to_right)
            def _():
                going_right(i, k, p, out.at[0, k, p], in_right.at[0, k, p]).wait_send()

            @pl.when(jnp.logical_and(to_left, c >= row))
            def _():
                going_left(i, k, p, out.at[0, k, p], in_left.at[0, k, p]).wait_send()

        each(body)

    def collect(i, k):
        par = i % 2
        goal = 2 * core + k

        @pl.when(jnp.logical_and(row < goal, row >= 1))
        def _():
            def body(p, c):
                came_right(i, k, p)

                @pl.when(c >= row)
                def _():
                    out[par, k, p] = (in_right[par, k, p].astype(f32) + term[k, p]).astype(bf16)
                    going_right(i, k, p, out.at[par, k, p], in_right.at[par, k, p]).start()

                @pl.when(c < row)
                def _():
                    going_right(i, k, p, in_right.at[par, k, p], in_right.at[par, k, p]).start()

            each(body)

        @pl.when(row > goal)
        def _():
            def body(p, c):
                @pl.when(c > row)
                def _():
                    came_left(i, k, p)
                    out[par, k, p] = (in_left[par, k, p].astype(f32) + term[k, p]).astype(bf16)
                    going_left(i, k, p, out.at[par, k, p], in_left.at[par, k, p]).start()

            each(body)

    def keep(i, k):
        par = i % 2
        goal = 2 * core + k

        @pl.when(row == goal)
        def _():
            def body(p, c):
                @pl.when(row >= 1)
                def _():
                    came_right(i, k, p)

                @pl.when(c > row)
                def _():
                    came_left(i, k, p)

                @pl.when(c < row)
                def _():
                    x[i, k, p] = in_right[par, k, p]

                @pl.when(c >= row)
                def _():
                    @pl.when(row >= 1)
                    def _():
                        term[k, p] = term[k, p] + in_right[par, k, p].astype(f32)

                    @pl.when(c > row)
                    def _():
                        term[k, p] = term[k, p] + in_left[par, k, p].astype(f32)

                    x[i, k, p] = term[k, p].astype(bf16)

            each(body)

    def far_copy(i, k, h):
        return remote(far_out.at[i - 1, k, h], far_in.at[i - 1, k, h], far_send.at[i - 1, k, h], far_recv.at[i - 1, k, h], far)

    def update(i, k):
        at = pair_index(i, i - 1)
        loaded("f", at)
        if i > 1:
            partial[k] = ahead[k * width : (k + 1) * width, :]
        else:
            partial[k] = jnp.zeros_like(partial[k])

        def body(p, c):
            came_last(i - 1, k, p, c)
            partial[k] += dot_t(x[i - 1, k, p], factor[at % factor_slots, p // 2, :, span(p)])

        each(body)
        for h in range(2):
            far_out[i - 1, k, h] = partial[k, :, h * (rows // 2) : (h + 1) * (rows // 2)].astype(bf16)
            far_copy(i, k, h).start()
        sent(i - 1, k)

    def look_ahead(i):
        for j in range(i - 1):
            at = pair_index(i, j)
            loaded("f", at)

            def body(p, c):
                value = dot_t(x[j, :, p].reshape(CHAINS * width, piece), factor[at % factor_slots, p // 2, :, span(p)])
                if j == 0:
                    @pl.when(p == 0)
                    def _():
                        ahead[...] = value

                    @pl.when(p > 0)
                    def _():
                        ahead[...] += value
                else:
                    ahead[...] += value

            each(body)

    owner = core == row // 2
    chain_at = lax.rem(row, 2)

    def give_copy(i, h):
        return remote(x.at[i, chain_at, 2 * (1 - core) + h], solved.at[i, h], give_send.at[i, h], give_recv.at[i, h], sibling)

    def give(i):
        @pl.when(owner)
        def _():
            for h in range(2):
                give_copy(i, h).start()
            for h in range(2):
                solved[i, h] = x[i, chain_at, 2 * core + h]

    def allow(n):
        pl.semaphore_signal(credit.at[n], inc=1, device_id=sibling, device_id_type=MESH)

    def refill(n, kind, at):
        pl.semaphore_wait(credit.at[n], 1)
        local_tile(kind, at).start()
        pushed_tile(kind, at).start()

    a, b = 0, 1
    turn(0)
    solve(0, a)
    solve(0, b)
    allow(0)
    turn(1)
    relay_first(0, a)
    relay_second(0, a)
    update(1, a)
    refill(0, "i", 3)
    for kind, at in late:
        pushed_tile(kind, at).start()
    relay_first(0, b)
    relay_second(0, b)
    for i in range(1, steps):
        solve(i, a)
        update(i, b)
        give(i - 1)
        if i == 1:
            allow(1)
        if i < last:
            relay_first(i, a)
            relay_second(i, a)
            solve(i, b)
            if i == 1:
                allow(2)
            turn(i + 1)
            look_ahead(i + 1)
            update(i + 1, a)
            if i == 1:
                refill(1, "f", factor_slots)
                refill(2, "i", 4)
            relay_first(i, b)
            relay_second(i, b)
        else:
            collect(i, a)
            solve(i, b)
            collect(i, b)
            keep(i, a)
            keep(i, b)
            give(i)
            sent(i, a)
            sent(i, b)

    @pl.when(owner)
    def _():
        for i in range(steps):
            for h in range(2):
                give_copy(i, h).wait_send()

    @pl.when(jnp.logical_not(owner))
    def _():
        for i in range(steps):
            for h in range(2):
                give_copy(i, h).wait_recv()

    for i in range(1, steps):
        for k in range(CHAINS):
            for h in range(2):
                far_copy(i, k, h).wait_send()
    for kind, at in tiles:
        pushed_tile(kind, at).wait_send()


def line_solve(factor_blocks, inverse_blocks, right_sides):
    steps, rows, angles = right_sides.shape
    pairs = factor_blocks.shape[0]
    col_rows = inverse_blocks.shape[1]
    width = angles // lax.axis_size("row")
    both = CHAINS * width
    half = rows // 2
    piece = col_rows // 2
    line = (2, CHAINS, PIECES, width, piece)
    dma = pltpu.SemaphoreType.DMA
    solved = pl.pallas_call(
        kernel,
        out_shape=jax.ShapeDtypeStruct((steps, 2, width, piece), bf16),
        in_specs=[pl.BlockSpec(memory_space=pl.ANY)] * 3,
        out_specs=pl.BlockSpec(memory_space=pltpu.VMEM),
        scratch_shapes=[
            pltpu.VMEM((pairs - 1, 2) + factor_blocks.shape[1:], bf16),
            pltpu.VMEM((INVERSE_SLOTS, 2) + inverse_blocks.shape[1:], bf16),
            pltpu.VMEM((steps, rows, both), bf16),
            pltpu.VMEM((steps, both, rows), bf16),
            pltpu.VMEM((steps, CHAINS, PIECES, width, piece), bf16),
            pltpu.VMEM(line, bf16),
            pltpu.VMEM(line, bf16),
            pltpu.VMEM(line, bf16),
            pltpu.VMEM((CHAINS, PIECES, width, piece), f32),
            pltpu.VMEM((CHAINS, width, rows), f32),
            pltpu.VMEM((both, rows), f32),
            pltpu.VMEM((steps - 1, CHAINS, 2, width, half), bf16),
            pltpu.VMEM((steps - 1, CHAINS, 2, width, half), bf16),
            pltpu.VMEM((CHAINS, width, rows), bf16),
            dma((pairs + 2 * steps,)),
            dma((pairs + steps,)),
            dma((pairs + steps,)),
            dma((steps - 1, CHAINS, 2)),
            dma((steps - 1, CHAINS, 2)),
            dma((steps, CHAINS, 2, PIECES)),
            dma((steps, CHAINS, 2, PIECES)),
            dma((steps, 2)),
            dma((steps, 2)),
            pltpu.SemaphoreType.REGULAR((3,)),
        ],
        compiler_params=pltpu.CompilerParams(
            collective_id=0, has_side_effects=True, vmem_limit_bytes=67043328
        ),
    )(factor_blocks, inverse_blocks, right_sides)
    return solved.transpose(0, 1, 3, 2).reshape(steps, col_rows, width)


def plain_solve(factor_blocks, inverse_blocks, right_sides):
    steps_total = right_sides.shape[0]
    solved = []
    outputs = []
    for block_row in range(steps_total):
        residual = right_sides[block_row].astype(jnp.float32)
        if block_row > 0:
            partial_value = jnp.zeros(residual.shape, jnp.float32)
            for column_index in range(block_row):
                partial_value = partial_value + jnp.dot(
                    factor_blocks[pair_index(block_row, column_index)],
                    solved[column_index],
                    preferred_element_type=jnp.float32,
                )
            residual = residual - lax.psum(partial_value, "col")
        residual_bf = residual.astype(jnp.bfloat16)
        term = jnp.dot(inverse_blocks[block_row], residual_bf, preferred_element_type=jnp.float32)
        share = lax.psum_scatter(term, "row", scatter_dimension=1, tiled=True).astype(jnp.bfloat16)
        outputs.append(share)
        if block_row + 1 < steps_total:
            solved.append(lax.all_gather(share, "row", axis=1, tiled=True))
    return jnp.stack(outputs, axis=0)


def solution(mesh):
    placed = (P("groups", "row", "col"), P("groups", "col", "row"), P("groups", "row", None))
    per_device = line_solve if mesh.shape["row"] == 4 and mesh.shape["col"] == 4 else plain_solve
    return jax.shard_map(
        per_device, mesh=mesh, in_specs=placed, out_specs=P("groups", "col", "row"), check_vma=False
    )
```

```python
import jax
import jax.numpy as jnp
from jax import lax
from jax.experimental import pallas as pl
from jax.experimental.pallas import tpu as pltpu
from jax.sharding import PartitionSpec as P

MESH = pl.DeviceIdType.MESH
CHAINS = 2
PIECES = 4
INVERSE_SLOTS = 3
MORE = 6
f32, bf16 = jnp.float32, jnp.bfloat16


def pair_index(block_row, column_index):
    return block_row * (block_row - 1) // 2 + column_index


def dot_t(a, b):
    return lax.dot_general(a, b, (((1,), (1,)), ((), ())), preferred_element_type=f32)


def kernel(
    factor_hbm, inverse_hbm, right_hbm, solved,
    factor, inverse, right, turned, x, in_right, in_left, out, term, partial, ahead, far_out, far_in, residual,
    load_sem, push_send, push_recv, far_send, far_recv, line_send, line_recv, give_send, give_recv, keep_sem, first_sem, credit,
):
    steps, width = solved.shape[:2]
    piece = x.shape[4]
    pairs = factor_hbm.shape[0]
    rows = right.shape[1]
    factor_slots = factor.shape[0]
    row = lax.axis_index("row")
    col = lax.axis_index("col")
    group = lax.axis_index("groups")
    core = lax.rem(col, 2)
    side = col // 2
    sibling = (group, row, col + 1 - 2 * core)
    far = (group, row, lax.rem(col + 2, 4))
    left = (group, jnp.maximum(row - 1, 0), col)
    right_dev = (group, jnp.minimum(row + 1, 3), col)
    last = steps - 1

    def remote(src, dst, send, recv, peer):
        return pltpu.make_async_remote_copy(
            src_ref=src, dst_ref=dst, send_sem=send, recv_sem=recv, device_id=peer, device_id_type=MESH
        )

    def span(p):
        return pl.ds(pl.multiple_of(lax.rem(p, 2) * piece, piece), piece)

    def local_tile(kind, at):
        if kind == "f":
            return pltpu.make_async_copy(factor_hbm.at[at], factor.at[at % factor_slots, core], load_sem.at[at])
        return pltpu.make_async_copy(inverse_hbm.at[at], inverse.at[at % INVERSE_SLOTS, core], load_sem.at[pairs + at])

    def pushed_tile(kind, at):
        if kind == "f":
            dst = factor.at[at % factor_slots, core]
            return remote(factor_hbm.at[at], dst, push_send.at[at], push_recv.at[at], sibling)
        dst = inverse.at[at % INVERSE_SLOTS, core]
        return remote(inverse_hbm.at[at], dst, push_send.at[pairs + at], push_recv.at[pairs + at], sibling)

    def landed_tile(kind, at):
        if kind == "f":
            dst = factor.at[at % factor_slots, 1 - core]
            return remote(factor_hbm.at[at], dst, push_send.at[at], push_recv.at[at], sibling)
        dst = inverse.at[at % INVERSE_SLOTS, 1 - core]
        return remote(inverse_hbm.at[at], dst, push_send.at[pairs + at], push_recv.at[pairs + at], sibling)

    tiles = [("i", 0)]
    for i in range(1, steps):
        tiles += [("f", pair_index(i, j)) for j in range(i)] + [("i", i)]
    fresh = [t for t in tiles if not (t[0] == "f" and t[1] >= factor_slots or t[0] == "i" and t[1] >= INVERSE_SLOTS)]
    early = [t for t in fresh if t[0] == "i" or t[1] < pair_index(4, 0)]
    late = [t for t in fresh if t not in early]
    ready = {tiles[0]}

    def loaded(kind, at):
        if (kind, at) not in ready:
            ready.add((kind, at))
            local_tile(kind, at).wait()
            landed_tile(kind, at).wait_recv()

    lanes = pl.ds(pl.multiple_of(core * CHAINS * width, CHAINS * width), CHAINS * width)

    def right_load(i):
        return pltpu.make_async_copy(right_hbm.at[i, :, lanes], right.at[i], load_sem.at[pairs + steps + i])

    def first_load(h):
        return pltpu.make_async_copy(inverse_hbm.at[0, span(h)], inverse.at[0, core, span(h)], first_sem.at[0, h])

    def first_push(h, par):
        return remote(inverse_hbm.at[0, span(h)], inverse.at[0, par, span(h)], first_sem.at[1, h], first_sem.at[2, h], sibling)

    right_load(0).start()
    for h in range(2):
        first_load(h).start()
    for i in range(1, steps):
        right_load(i).start()
    for kind, at in fresh[1:]:
        local_tile(kind, at).start()

    barrier = pltpu.get_barrier_semaphore()
    for peer in (sibling, far):
        pl.semaphore_signal(barrier, inc=1, device_id=peer, device_id_type=MESH)

    @pl.when(row > 0)
    def _():
        pl.semaphore_signal(barrier, inc=1, device_id=left, device_id_type=MESH)

    @pl.when(row < 3)
    def _():
        pl.semaphore_signal(barrier, inc=1, device_id=right_dev, device_id_type=MESH)

    @pl.when(jnp.logical_or(row == 0, row == 3))
    def _():
        pl.semaphore_wait(barrier, 3)

    @pl.when(jnp.logical_and(row > 0, row < 3))
    def _():
        pl.semaphore_wait(barrier, 4)

    for h in range(2):
        first_push(h, core).start()
    for kind, at in early[1:]:
        pushed_tile(kind, at).start()

    def turn(i):
        right_load(i).wait()
        turned[i] = right[i].T

    def going_right(i, k, p, src, dst):
        return remote(src, dst, line_send.at[i, k, 0, p], line_recv.at[i, k, 0, p], right_dev)

    def going_left(i, k, p, src, dst):
        return remote(src, dst, line_send.at[i, k, 1, p], line_recv.at[i, k, 1, p], left)

    def each(body, start=0, turned_by=0):
        def step(p, carry):
            p = lax.rem(p + turned_by, PIECES)
            body(p, 2 * side + p // 2)
            return carry

        lax.fori_loop(start, PIECES, step, 0)

    def order(i):
        if i == 0:
            return 2 * core
        return 2 * (1 - core) if i == last else 0

    def solve(i, k):
        chain = slice(k * width, (k + 1) * width)
        if i == 0:
            residual[k] = turned[0, chain, :]
        else:
            for h in range(2):
                cols = slice(h * (rows // 2), (h + 1) * (rows // 2))
                far_copy(i, k, h).wait_recv()
                total = partial[k, :, cols] + far_in[i - 1, k, h].astype(f32)
                residual[k, :, cols] = (turned[i, chain, cols].astype(f32) - total).astype(bf16)
        loaded("i", i)
        par = i % 2
        goal = 2 * core + k
        if i >= 2:
            sent(i - 2, k)

        def body(p, c):
            if i == 0 and k == 0:
                @pl.when(p // 2 == core)
                def _():
                    first_load(lax.rem(p, 2)).wait()

                @pl.when(p // 2 != core)
                def _():
                    first_push(lax.rem(p, 2), 1 - core).wait_recv()

            @pl.when(c >= row)
            def _():
                value = dot_t(residual[k], inverse[i % INVERSE_SLOTS, p // 2, span(p), :])
                term[k, p] = value
                out[par, k, p] = value.astype(bf16)
                if i < last:
                    @pl.when(jnp.logical_and(row == 0, c == 0))
                    def _():
                        x[i, k, p] = value.astype(bf16)
                        going_right(i, k, p, x.at[i, k, p], x.at[i, k, p]).start()

                    @pl.when(jnp.logical_and(row == 0, c > 0))
                    def _():
                        going_right(i, k, p, out.at[par, k, p], in_right.at[par, k, p]).start()

                    @pl.when(jnp.logical_and(row >= 2, c == row))
                    def _():
                        going_left(i, k, p, out.at[par, k, p], in_left.at[par, k, p]).start()
                else:
                    @pl.when(jnp.logical_and(row == 0, goal > 0))
                    def _():
                        going_right(i, k, p, out.at[par, k, p], in_right.at[par, k, p]).start()

                    @pl.when(jnp.logical_and(row > goal, c == row))
                    def _():
                        going_left(i, k, p, out.at[par, k, p], in_left.at[par, k, p]).start()

        each(body, 0, order(i))

    def came_right(i, k, p):
        going_right(i, k, p, out.at[0, k, p], in_right.at[0, k, p]).wait_recv()

    def came_left(i, k, p):
        going_left(i, k, p, out.at[0, k, p], in_left.at[0, k, p]).wait_recv()

    def relay_first(i, k, p, c):
        par = i % 2

        @pl.when(row == 1)
        def _():
            came_right(i, k, p)

            @pl.when(c == 0)
            def _():
                going_right(i, k, p, x.at[i, k, p], x.at[i, k, p]).start()

            @pl.when(c == 1)
            def _():
                x[i, k, p] = (in_right[par, k, p].astype(f32) + term[k, p]).astype(bf16)
                going_right(i, k, p, x.at[i, k, p], x.at[i, k, p]).start()
                going_left(i, k, p, x.at[i, k, p], x.at[i, k, p]).start()

            @pl.when(c >= 2)
            def _():
                out[par, k, p] = (in_right[par, k, p].astype(f32) + term[k, p]).astype(bf16)
                going_right(i, k, p, out.at[par, k, p], in_right.at[par, k, p]).start()

        @pl.when(jnp.logical_and(row == 2, c == 3))
        def _():
            came_left(i, k, p)
            out[par, k, p] = (in_left[par, k, p].astype(f32) + term[k, p]).astype(bf16)
            going_left(i, k, p, out.at[par, k, p], in_left.at[par, k, p]).start()

    def relay_second(i, k, p, c):
        par = i % 2

        @pl.when(jnp.logical_and(row == 1, c >= 2))
        def _():
            came_left(i, k, p)
            x[i, k, p] = (out[par, k, p].astype(f32) + in_left[par, k, p].astype(f32)).astype(bf16)
            going_left(i, k, p, x.at[i, k, p], x.at[i, k, p]).start()

        @pl.when(row == 2)
        def _():
            came_right(i, k, p)

            @pl.when(c >= 2)
            def _():
                x[i, k, p] = (out[par, k, p].astype(f32) + in_right[par, k, p].astype(f32)).astype(bf16)

            going_right(i, k, p, x.at[i, k, p], x.at[i, k, p]).start()

    def came_last(i, k, p, c):
        @pl.when(jnp.logical_and(row == 0, c >= 1))
        def _():
            came_left(i, k, p)

        @pl.when(row == 3)
        def _():
            came_right(i, k, p)

    def sent(i, k):
        goal = 2 * core + k
        to_right = row < 3 if i < last else row < goal
        to_left = row > 0 if i < last else row > goal

        def body(p, c):
            @pl.when(to_right)
            def _():
                going_right(i, k, p, out.at[0, k, p], in_right.at[0, k, p]).wait_send()

            @pl.when(jnp.logical_and(to_left, c >= row))
            def _():
                going_left(i, k, p, out.at[0, k, p], in_left.at[0, k, p]).wait_send()

        each(body, 0, order(i))

    def collect(i, k):
        par = i % 2
        goal = 2 * core + k

        @pl.when(jnp.logical_and(row < goal, row >= 1))
        def _():
            def body(p, c):
                came_right(i, k, p)

                @pl.when(c >= row)
                def _():
                    out[par, k, p] = (in_right[par, k, p].astype(f32) + term[k, p]).astype(bf16)
                    going_right(i, k, p, out.at[par, k, p], in_right.at[par, k, p]).start()

                @pl.when(c < row)
                def _():
                    going_right(i, k, p, in_right.at[par, k, p], in_right.at[par, k, p]).start()

            each(body, 0, order(i))

        @pl.when(row > goal)
        def _():
            def body(p, c):
                @pl.when(c > row)
                def _():
                    came_left(i, k, p)
                    out[par, k, p] = (in_left[par, k, p].astype(f32) + term[k, p]).astype(bf16)
                    going_left(i, k, p, out.at[par, k, p], in_left.at[par, k, p]).start()

            each(body, 0, order(i))

    def keep(i, k):
        par = i % 2
        goal = 2 * core + k

        @pl.when(row == goal)
        def _():
            def body(p, c):
                @pl.when(row >= 1)
                def _():
                    came_right(i, k, p)

                @pl.when(c > row)
                def _():
                    came_left(i, k, p)

                @pl.when(c < row)
                def _():
                    x[i, k, p] = in_right[par, k, p]

                @pl.when(c >= row)
                def _():
                    @pl.when(row >= 1)
                    def _():
                        term[k, p] = term[k, p] + in_right[par, k, p].astype(f32)

                    @pl.when(c > row)
                    def _():
                        term[k, p] = term[k, p] + in_left[par, k, p].astype(f32)

                    x[i, k, p] = term[k, p].astype(bf16)

                @pl.when(p // 2 == core)
                def _():
                    keep_copy(i, lax.rem(p, 2)).start()

                @pl.when(p // 2 != core)
                def _():
                    give_copy(i, lax.rem(p, 2)).start()

            each(body, 0, order(i))

    def far_copy(i, k, h):
        return remote(far_out.at[i - 1, k, h], far_in.at[i - 1, k, h], far_send.at[i - 1, k, h], far_recv.at[i - 1, k, h], far)

    def update(i, k):
        at = pair_index(i, i - 1)
        loaded("f", at)
        if i > 1:
            partial[k] = ahead[i - 2, k * width : (k + 1) * width, :]
        else:
            partial[k] = jnp.zeros_like(partial[k])

        def body(p, c):
            came_last(i - 1, k, p, c)
            partial[k] += dot_t(x[i - 1, k, p], factor[at % factor_slots, p // 2, :, span(p)])

        each(body, 0, order(i - 1))
        for h in range(2):
            far_out[i - 1, k, h] = partial[k, :, h * (rows // 2) : (h + 1) * (rows // 2)].astype(bf16)
            far_copy(i, k, h).start()

    begun = set()

    def look_ahead(i, j, par, h):
        at = pair_index(i, j)
        loaded("f", at)
        known = [x[j, :, 2 * par + q].reshape(CHAINS * width, piece) for q in range(2)]
        cols = slice(h * piece, (h + 1) * piece)
        value = dot_t(jnp.concatenate(known, axis=1), factor[at % factor_slots, par, cols, :])
        if (i, h) in begun:
            value = value + ahead[i - 2, :, cols]
        begun.add((i, h))
        ahead[i - 2, :, cols] = value

    waiting = [(i, j, par, h) for i in range(2, steps) for j in range(i - 1) for par in range(2) for h in range(2)]

    def take(units):
        for unit in units:
            waiting.remove(unit)
        return units

    def look_due(i):
        return take([u for u in waiting if u[0] == i + 1])

    def look_more(i):
        return take([u for u in waiting if u[0] > i + 1 and u[1] < i][:MORE])

    def relay(i, k, units):
        units = list(units)
        for stage in (relay_first, relay_second):
            for q in range(PIECES):
                p = lax.rem(q + order(i), PIECES)
                stage(i, k, p, 2 * side + p // 2)
                if units:
                    look_ahead(*units.pop(0))
        for unit in units:
            look_ahead(*unit)

    owner = core == row // 2
    chain_at = lax.rem(row, 2)

    def give_copy(i, h):
        p = 2 * (1 - core) + h
        return remote(x.at[i, chain_at, p], solved.at[i, :, span(h)], give_send.at[i, h], give_recv.at[i, h], sibling)

    def keep_copy(i, h):
        return pltpu.make_async_copy(x.at[i, chain_at, 2 * core + h], solved.at[i, :, span(h)], keep_sem.at[i, h])

    def give(i):
        @pl.when(owner)
        def _():
            for h in range(2):
                give_copy(i, h).start()
                keep_copy(i, h).start()

    def allow(n):
        pl.semaphore_signal(credit.at[n], inc=1, device_id=sibling, device_id_type=MESH)

    def refill(n, kind, at):
        pl.semaphore_wait(credit.at[n], 1)
        local_tile(kind, at).start()
        pushed_tile(kind, at).start()

    def settle_gives(which):
        @pl.when(owner)
        def _():
            for i in which:
                for h in range(2):
                    give_copy(i, h).wait_send()
                    keep_copy(i, h).wait()

        @pl.when(jnp.logical_not(owner))
        def _():
            for i in which:
                for h in range(2):
                    give_copy(i, h).wait_recv()

    def settle():
        settle_gives(range(last))
        for k in range(CHAINS):
            sent(last - 1, k)
        for i in range(1, steps):
            for k in range(CHAINS):
                for h in range(2):
                    far_copy(i, k, h).wait_send()
        for h in range(2):
            first_push(h, core).wait_send()
        for kind, at in tiles[1:]:
            pushed_tile(kind, at).wait_send()

    a, b = 0, 1
    turn(0)
    solve(0, a)
    solve(0, b)
    allow(0)
    turn(1)
    relay(0, a, [])
    update(1, a)
    refill(0, "i", 3)
    for kind, at in late:
        pushed_tile(kind, at).start()
    relay(0, b, [])
    for i in range(1, steps):
        solve(i, a)
        update(i, b)
        give(i - 1)
        if i == 1:
            allow(1)
        if i < last:
            relay(i, a, look_due(i))
            solve(i, b)
            if i == 1:
                allow(2)
            turn(i + 1)
            update(i + 1, a)
            if i == 1:
                refill(1, "f", factor_slots)
                refill(2, "i", 4)
            relay(i, b, look_more(i))
        else:
            collect(i, a)
            solve(i, b)
            collect(i, b)
            settle()
            keep(i, a)
            keep(i, b)

    settle_gives([last])
    for k in range(CHAINS):
        sent(last, k)


def line_solve(factor_blocks, inverse_blocks, right_sides):
    steps, rows, angles = right_sides.shape
    pairs = factor_blocks.shape[0]
    col_rows = inverse_blocks.shape[1]
    width = angles // lax.axis_size("row")
    both = CHAINS * width
    half = rows // 2
    piece = col_rows // 2
    line = (2, CHAINS, PIECES, width, piece)
    dma = pltpu.SemaphoreType.DMA
    solved = pl.pallas_call(
        kernel,
        out_shape=jax.ShapeDtypeStruct((steps, width, col_rows), bf16),
        in_specs=[pl.BlockSpec(memory_space=pl.ANY)] * 3,
        out_specs=pl.BlockSpec(memory_space=pl.ANY),
        scratch_shapes=[
            pltpu.VMEM((pairs - 1, 2) + factor_blocks.shape[1:], bf16),
            pltpu.VMEM((INVERSE_SLOTS, 2) + inverse_blocks.shape[1:], bf16),
            pltpu.VMEM((steps, rows, both), bf16),
            pltpu.VMEM((steps, both, rows), bf16),
            pltpu.VMEM((steps, CHAINS, PIECES, width, piece), bf16),
            pltpu.VMEM(line, bf16),
            pltpu.VMEM(line, bf16),
            pltpu.VMEM(line, bf16),
            pltpu.VMEM((CHAINS, PIECES, width, piece), f32),
            pltpu.VMEM((CHAINS, width, rows), f32),
            pltpu.VMEM((steps - 2, both, rows), f32),
            pltpu.VMEM((steps - 1, CHAINS, 2, width, half), bf16),
            pltpu.VMEM((steps - 1, CHAINS, 2, width, half), bf16),
            pltpu.VMEM((CHAINS, width, rows), bf16),
            dma((pairs + 2 * steps,)),
            dma((pairs + steps,)),
            dma((pairs + steps,)),
            dma((steps - 1, CHAINS, 2)),
            dma((steps - 1, CHAINS, 2)),
            dma((steps, CHAINS, 2, PIECES)),
            dma((steps, CHAINS, 2, PIECES)),
            dma((steps, 2)),
            dma((steps, 2)),
            dma((steps, 2)),
            dma((3, 2)),
            pltpu.SemaphoreType.REGULAR((3,)),
        ],
        compiler_params=pltpu.CompilerParams(
            collective_id=0, has_side_effects=True, vmem_limit_bytes=67043328
        ),
    )(factor_blocks, inverse_blocks, right_sides)
    return solved.transpose(0, 2, 1)


def plain_solve(factor_blocks, inverse_blocks, right_sides):
    steps_total = right_sides.shape[0]
    solved = []
    outputs = []
    for block_row in range(steps_total):
        residual = right_sides[block_row].astype(jnp.float32)
        if block_row > 0:
            partial_value = jnp.zeros(residual.shape, jnp.float32)
            for column_index in range(block_row):
                partial_value = partial_value + jnp.dot(
                    factor_blocks[pair_index(block_row, column_index)],
                    solved[column_index],
                    preferred_element_type=jnp.float32,
                )
            residual = residual - lax.psum(partial_value, "col")
        residual_bf = residual.astype(jnp.bfloat16)
        term = jnp.dot(inverse_blocks[block_row], residual_bf, preferred_element_type=jnp.float32)
        share = lax.psum_scatter(term, "row", scatter_dimension=1, tiled=True).astype(jnp.bfloat16)
        outputs.append(share)
        if block_row + 1 < steps_total:
            solved.append(lax.all_gather(share, "row", axis=1, tiled=True))
    return jnp.stack(outputs, axis=0)


def solution(mesh):
    placed = (P("groups", "row", "col"), P("groups", "col", "row"), P("groups", "row", None))
    per_device = line_solve if mesh.shape["row"] == 4 and mesh.shape["col"] == 4 else plain_solve
    return jax.shard_map(
        per_device, mesh=mesh, in_specs=placed, out_specs=P("groups", "col", "row"), check_vma=False
    )
```

```python
import jax
import jax.numpy as jnp
from jax import lax
from jax.experimental import pallas as pl
from jax.experimental.pallas import tpu as pltpu
from jax.sharding import PartitionSpec as P

MESH = pl.DeviceIdType.MESH
CHAINS = 2
PIECES = 4
INVERSE_SLOTS = 3
MORE = 6
f32, bf16 = jnp.float32, jnp.bfloat16


def pair_index(block_row, column_index):
    return block_row * (block_row - 1) // 2 + column_index


def dot_t(a, b):
    return lax.dot_general(a, b, (((1,), (1,)), ((), ())), preferred_element_type=f32)


def kernel(
    factor_hbm, inverse_hbm, right_hbm, solved,
    factor, inverse, right, turned, x, in_right, in_left, out, term, partial, ahead, far_out, far_in, residual,
    load_sem, push_send, push_recv, far_send, far_recv, line_send, line_recv, give_send, give_recv, keep_sem, first_sem, credit,
):
    steps, width = solved.shape[:2]
    piece = x.shape[4]
    pairs = factor_hbm.shape[0]
    rows = right.shape[1]
    factor_slots = factor.shape[0]
    row = lax.axis_index("row")
    col = lax.axis_index("col")
    group = lax.axis_index("groups")
    core = lax.rem(col, 2)
    side = col // 2
    sibling = (group, row, col + 1 - 2 * core)
    far = (group, row, lax.rem(col + 2, 4))
    left = (group, jnp.maximum(row - 1, 0), col)
    right_dev = (group, jnp.minimum(row + 1, 3), col)
    last = steps - 1

    def remote(src, dst, send, recv, peer):
        return pltpu.make_async_remote_copy(
            src_ref=src, dst_ref=dst, send_sem=send, recv_sem=recv, device_id=peer, device_id_type=MESH
        )

    def span(p):
        return pl.ds(pl.multiple_of(lax.rem(p, 2) * piece, piece), piece)

    def local_tile(kind, at):
        if kind == "f":
            return pltpu.make_async_copy(factor_hbm.at[at], factor.at[at % factor_slots, core], load_sem.at[at])
        return pltpu.make_async_copy(inverse_hbm.at[at], inverse.at[at % INVERSE_SLOTS, core], load_sem.at[pairs + at])

    def pushed_tile(kind, at):
        if kind == "f":
            dst = factor.at[at % factor_slots, core]
            return remote(factor_hbm.at[at], dst, push_send.at[at], push_recv.at[at], sibling)
        dst = inverse.at[at % INVERSE_SLOTS, core]
        return remote(inverse_hbm.at[at], dst, push_send.at[pairs + at], push_recv.at[pairs + at], sibling)

    def landed_tile(kind, at):
        if kind == "f":
            dst = factor.at[at % factor_slots, 1 - core]
            return remote(factor_hbm.at[at], dst, push_send.at[at], push_recv.at[at], sibling)
        dst = inverse.at[at % INVERSE_SLOTS, 1 - core]
        return remote(inverse_hbm.at[at], dst, push_send.at[pairs + at], push_recv.at[pairs + at], sibling)

    tiles = [("i", 0)]
    for i in range(1, steps):
        tiles += [("f", pair_index(i, j)) for j in range(i)] + [("i", i)]
    fresh = [t for t in tiles if not (t[0] == "f" and t[1] >= factor_slots or t[0] == "i" and t[1] >= INVERSE_SLOTS)]
    early = [t for t in fresh if t[0] == "i" or t[1] < pair_index(4, 0)]
    late = [t for t in fresh if t not in early]
    ready = {tiles[0]}

    def loaded(kind, at):
        if (kind, at) not in ready:
            ready.add((kind, at))
            local_tile(kind, at).wait()
            landed_tile(kind, at).wait_recv()

    lanes = pl.ds(pl.multiple_of(core * CHAINS * width, CHAINS * width), CHAINS * width)

    def right_load(i):
        return pltpu.make_async_copy(right_hbm.at[i, :, lanes], right.at[i], load_sem.at[pairs + steps + i])

    def first_load(h):
        return pltpu.make_async_copy(inverse_hbm.at[0, span(h)], inverse.at[0, core, span(h)], first_sem.at[0, h])

    def first_push(h, par):
        return remote(inverse_hbm.at[0, span(h)], inverse.at[0, par, span(h)], first_sem.at[1, h], first_sem.at[2, h], sibling)

    right_load(0).start()
    for h in range(2):
        first_load(h).start()
    for i in range(1, steps):
        right_load(i).start()
    for kind, at in fresh[1:]:
        local_tile(kind, at).start()

    barrier = pltpu.get_barrier_semaphore()
    for peer in (sibling, far):
        pl.semaphore_signal(barrier, inc=1, device_id=peer, device_id_type=MESH)

    @pl.when(row > 0)
    def _():
        pl.semaphore_signal(barrier, inc=1, device_id=left, device_id_type=MESH)

    @pl.when(row < 3)
    def _():
        pl.semaphore_signal(barrier, inc=1, device_id=right_dev, device_id_type=MESH)

    @pl.when(jnp.logical_or(row == 0, row == 3))
    def _():
        pl.semaphore_wait(barrier, 3)

    @pl.when(jnp.logical_and(row > 0, row < 3))
    def _():
        pl.semaphore_wait(barrier, 4)

    for h in range(2):
        first_push(h, core).start()
    for kind, at in early[1:]:
        pushed_tile(kind, at).start()

    def turn(i):
        right_load(i).wait()
        turned[i] = right[i].T

    def going_right(i, k, p, src, dst):
        return remote(src, dst, line_send.at[i % 2, k, 0, p], line_recv.at[i % 2, k, 0, p], right_dev)

    def going_left(i, k, p, src, dst):
        return remote(src, dst, line_send.at[i % 2, k, 1, p], line_recv.at[i % 2, k, 1, p], left)

    def each(body, start=0, turned_by=0):
        def step(p, carry):
            p = lax.rem(p + turned_by, PIECES)
            body(p, 2 * side + p // 2)
            return carry

        lax.fori_loop(start, PIECES, step, 0)

    def order(i):
        if i == 0:
            return 2 * core
        return 2 * (1 - core) if i == last else 0

    def solve(i, k):
        chain = slice(k * width, (k + 1) * width)
        if i == 0:
            residual[k] = turned[0, chain, :]
        else:
            for h in range(2):
                cols = slice(h * (rows // 2), (h + 1) * (rows // 2))
                far_copy(i, k, h).wait_recv()
                total = partial[k, :, cols] + far_in[i - 1, k, h].astype(f32)
                residual[k, :, cols] = (turned[i, chain, cols].astype(f32) - total).astype(bf16)
        loaded("i", i)
        par = i % 2
        goal = 2 * core + k
        if i >= 2:
            sent(i - 2, k)

        def body(p, c):
            if i == 0 and k == 0:
                @pl.when(p // 2 == core)
                def _():
                    first_load(lax.rem(p, 2)).wait()

                @pl.when(p // 2 != core)
                def _():
                    first_push(lax.rem(p, 2), 1 - core).wait_recv()

            @pl.when(c >= row)
            def _():
                value = dot_t(residual[k], inverse[i % INVERSE_SLOTS, p // 2, span(p), :])
                term[k, p] = value
                out[par, k, p] = value.astype(bf16)
                if i < last:
                    @pl.when(jnp.logical_and(row == 0, c == 0))
                    def _():
                        x[i, k, p] = value.astype(bf16)
                        going_right(i, k, p, x.at[i, k, p], x.at[i, k, p]).start()

                    @pl.when(jnp.logical_and(row == 0, c > 0))
                    def _():
                        going_right(i, k, p, out.at[par, k, p], in_right.at[par, k, p]).start()

                    @pl.when(jnp.logical_and(row >= 2, c == row))
                    def _():
                        going_left(i, k, p, out.at[par, k, p], in_left.at[par, k, p]).start()
                else:
                    @pl.when(jnp.logical_and(row == 0, goal > 0))
                    def _():
                        going_right(i, k, p, out.at[par, k, p], in_right.at[par, k, p]).start()

                    @pl.when(jnp.logical_and(row > goal, c == row))
                    def _():
                        going_left(i, k, p, out.at[par, k, p], in_left.at[par, k, p]).start()

        each(body, 0, order(i))

    def came_right(i, k, p):
        going_right(i, k, p, out.at[0, k, p], in_right.at[0, k, p]).wait_recv()

    def came_left(i, k, p):
        going_left(i, k, p, out.at[0, k, p], in_left.at[0, k, p]).wait_recv()

    def relay_first(i, k, p, c):
        par = i % 2

        @pl.when(row == 1)
        def _():
            came_right(i, k, p)

            @pl.when(c == 0)
            def _():
                going_right(i, k, p, x.at[i, k, p], x.at[i, k, p]).start()

            @pl.when(c == 1)
            def _():
                x[i, k, p] = (in_right[par, k, p].astype(f32) + term[k, p]).astype(bf16)
                going_right(i, k, p, x.at[i, k, p], x.at[i, k, p]).start()
                going_left(i, k, p, x.at[i, k, p], x.at[i, k, p]).start()

            @pl.when(c >= 2)
            def _():
                out[par, k, p] = (in_right[par, k, p].astype(f32) + term[k, p]).astype(bf16)
                going_right(i, k, p, out.at[par, k, p], in_right.at[par, k, p]).start()

        @pl.when(jnp.logical_and(row == 2, c == 3))
        def _():
            came_left(i, k, p)
            out[par, k, p] = (in_left[par, k, p].astype(f32) + term[k, p]).astype(bf16)
            going_left(i, k, p, out.at[par, k, p], in_left.at[par, k, p]).start()

    def relay_second(i, k, p, c):
        par = i % 2

        @pl.when(jnp.logical_and(row == 1, c >= 2))
        def _():
            came_left(i, k, p)
            x[i, k, p] = (out[par, k, p].astype(f32) + in_left[par, k, p].astype(f32)).astype(bf16)
            going_left(i, k, p, x.at[i, k, p], x.at[i, k, p]).start()

        @pl.when(row == 2)
        def _():
            came_right(i, k, p)

            @pl.when(c >= 2)
            def _():
                x[i, k, p] = (out[par, k, p].astype(f32) + in_right[par, k, p].astype(f32)).astype(bf16)

            going_right(i, k, p, x.at[i, k, p], x.at[i, k, p]).start()

    def came_last(i, k, p, c):
        @pl.when(jnp.logical_and(row == 0, c >= 1))
        def _():
            came_left(i, k, p)

        @pl.when(row == 3)
        def _():
            came_right(i, k, p)

    def sent(i, k):
        goal = 2 * core + k
        to_right = row < 3 if i < last else row < goal
        to_left = row > 0 if i < last else row > goal

        def body(p, c):
            @pl.when(to_right)
            def _():
                going_right(i, k, p, out.at[0, k, p], in_right.at[0, k, p]).wait_send()

            @pl.when(jnp.logical_and(to_left, c >= row))
            def _():
                going_left(i, k, p, out.at[0, k, p], in_left.at[0, k, p]).wait_send()

        each(body, 0, order(i))

    def collect(i, k):
        par = i % 2
        goal = 2 * core + k

        @pl.when(jnp.logical_and(row < goal, row >= 1))
        def _():
            def body(p, c):
                came_right(i, k, p)

                @pl.when(c >= row)
                def _():
                    out[par, k, p] = (in_right[par, k, p].astype(f32) + term[k, p]).astype(bf16)
                    going_right(i, k, p, out.at[par, k, p], in_right.at[par, k, p]).start()

                @pl.when(c < row)
                def _():
                    going_right(i, k, p, in_right.at[par, k, p], in_right.at[par, k, p]).start()

            each(body, 0, order(i))

        @pl.when(row > goal)
        def _():
            def body(p, c):
                @pl.when(c > row)
                def _():
                    came_left(i, k, p)
                    out[par, k, p] = (in_left[par, k, p].astype(f32) + term[k, p]).astype(bf16)
                    going_left(i, k, p, out.at[par, k, p], in_left.at[par, k, p]).start()

            each(body, 0, order(i))

    def keep(i, k):
        par = i % 2
        goal = 2 * core + k

        @pl.when(row == goal)
        def _():
            def body(p, c):
                @pl.when(row >= 1)
                def _():
                    came_right(i, k, p)

                @pl.when(c > row)
                def _():
                    came_left(i, k, p)

                @pl.when(c < row)
                def _():
                    x[i, k, p] = in_right[par, k, p]

                @pl.when(c >= row)
                def _():
                    @pl.when(row >= 1)
                    def _():
                        term[k, p] = term[k, p] + in_right[par, k, p].astype(f32)

                    @pl.when(c > row)
                    def _():
                        term[k, p] = term[k, p] + in_left[par, k, p].astype(f32)

                    x[i, k, p] = term[k, p].astype(bf16)

                @pl.when(p // 2 == core)
                def _():
                    keep_copy(i, lax.rem(p, 2)).start()

                @pl.when(p // 2 != core)
                def _():
                    give_copy(i, lax.rem(p, 2)).start()

            each(body, 0, order(i))

    def far_copy(i, k, h):
        return remote(far_out.at[i - 1, k, h], far_in.at[i - 1, k, h], far_send.at[i % 2, k, h], far_recv.at[i % 2, k, h], far)

    def update(i, k):
        at = pair_index(i, i - 1)
        loaded("f", at)
        if i > 1:
            partial[k] = ahead[i - 2, k * width : (k + 1) * width, :]
        else:
            partial[k] = jnp.zeros_like(partial[k])

        def body(p, c):
            came_last(i - 1, k, p, c)
            partial[k] += dot_t(x[i - 1, k, p], factor[at % factor_slots, p // 2, :, span(p)])

        each(body, 0, order(i - 1))
        for h in range(2):
            if i > 2:
                far_copy(i - 2, k, h).wait_send()
            far_out[i - 1, k, h] = partial[k, :, h * (rows // 2) : (h + 1) * (rows // 2)].astype(bf16)
            far_copy(i, k, h).start()

    begun = set()

    def look_ahead(i, j, par, h):
        at = pair_index(i, j)
        loaded("f", at)
        known = [x[j, :, 2 * par + q].reshape(CHAINS * width, piece) for q in range(2)]
        cols = slice(h * piece, (h + 1) * piece)
        value = dot_t(jnp.concatenate(known, axis=1), factor[at % factor_slots, par, cols, :])
        if (i, h) in begun:
            value = value + ahead[i - 2, :, cols]
        begun.add((i, h))
        ahead[i - 2, :, cols] = value

    waiting = [(i, j, par, h) for i in range(2, steps) for j in range(i - 1) for par in range(2) for h in range(2)]

    def take(units):
        for unit in units:
            waiting.remove(unit)
        return units

    def look_due(i):
        return take([u for u in waiting if u[0] == i + 1])

    def look_more(i):
        return take([u for u in waiting if u[0] > i + 1 and u[1] < i][:MORE])

    def relay(i, k, units):
        units = list(units)
        for stage in (relay_first, relay_second):
            for q in range(PIECES):
                p = lax.rem(q + order(i), PIECES)
                stage(i, k, p, 2 * side + p // 2)
                if units:
                    look_ahead(*units.pop(0))
        for unit in units:
            look_ahead(*unit)

    owner = core == row // 2
    chain_at = lax.rem(row, 2)

    def give_copy(i, h):
        p = 2 * (1 - core) + h
        return remote(x.at[i, chain_at, p], solved.at[i, :, span(h)], give_send.at[i, h], give_recv.at[i, h], sibling)

    def keep_copy(i, h):
        return pltpu.make_async_copy(x.at[i, chain_at, 2 * core + h], solved.at[i, :, span(h)], keep_sem.at[i, h])

    def give(i):
        @pl.when(owner)
        def _():
            for h in range(2):
                give_copy(i, h).start()
                keep_copy(i, h).start()

    def allow(n):
        pl.semaphore_signal(credit.at[n], inc=1, device_id=sibling, device_id_type=MESH)

    def refill(n, kind, at):
        pl.semaphore_wait(credit.at[n], 1)
        local_tile(kind, at).start()
        pushed_tile(kind, at).start()

    def settle_gives(which):
        @pl.when(owner)
        def _():
            for i in which:
                for h in range(2):
                    give_copy(i, h).wait_send()
                    keep_copy(i, h).wait()

        @pl.when(jnp.logical_not(owner))
        def _():
            for i in which:
                for h in range(2):
                    give_copy(i, h).wait_recv()

    def settle():
        settle_gives(range(last))
        for k in range(CHAINS):
            sent(last - 1, k)
        for i in range(steps - 2, steps):
            for k in range(CHAINS):
                for h in range(2):
                    far_copy(i, k, h).wait_send()
        for h in range(2):
            first_push(h, core).wait_send()
        for kind, at in tiles[1:]:
            pushed_tile(kind, at).wait_send()

    a, b = 0, 1
    turn(0)
    solve(0, a)
    solve(0, b)
    allow(0)
    turn(1)
    relay(0, a, [])
    update(1, a)
    refill(0, "i", 3)
    for kind, at in late:
        pushed_tile(kind, at).start()
    relay(0, b, [])
    for i in range(1, steps):
        solve(i, a)
        update(i, b)
        give(i - 1)
        if i == 1:
            allow(1)
        if i < last:
            relay(i, a, look_due(i))
            solve(i, b)
            if i == 1:
                allow(2)
            turn(i + 1)
            update(i + 1, a)
            if i == 1:
                refill(1, "f", factor_slots)
                refill(2, "i", 4)
            relay(i, b, look_more(i))
        else:
            collect(i, a)
            solve(i, b)
            collect(i, b)
            settle()
            keep(i, a)
            keep(i, b)

    settle_gives([last])
    for k in range(CHAINS):
        sent(last, k)


def line_solve(factor_blocks, inverse_blocks, right_sides):
    steps, rows, angles = right_sides.shape
    pairs = factor_blocks.shape[0]
    col_rows = inverse_blocks.shape[1]
    width = angles // lax.axis_size("row")
    both = CHAINS * width
    half = rows // 2
    piece = col_rows // 2
    line = (2, CHAINS, PIECES, width, piece)
    dma = pltpu.SemaphoreType.DMA
    solved = pl.pallas_call(
        kernel,
        out_shape=jax.ShapeDtypeStruct((steps, width, col_rows), bf16),
        in_specs=[pl.BlockSpec(memory_space=pl.ANY)] * 3,
        out_specs=pl.BlockSpec(memory_space=pl.ANY),
        scratch_shapes=[
            pltpu.VMEM((pairs - 1, 2) + factor_blocks.shape[1:], bf16),
            pltpu.VMEM((INVERSE_SLOTS, 2) + inverse_blocks.shape[1:], bf16),
            pltpu.VMEM((steps, rows, both), bf16),
            pltpu.VMEM((steps, both, rows), bf16),
            pltpu.VMEM((steps, CHAINS, PIECES, width, piece), bf16),
            pltpu.VMEM(line, bf16),
            pltpu.VMEM(line, bf16),
            pltpu.VMEM(line, bf16),
            pltpu.VMEM((CHAINS, PIECES, width, piece), f32),
            pltpu.VMEM((CHAINS, width, rows), f32),
            pltpu.VMEM((steps - 2, both, rows), f32),
            pltpu.VMEM((steps - 1, CHAINS, 2, width, half), bf16),
            pltpu.VMEM((steps - 1, CHAINS, 2, width, half), bf16),
            pltpu.VMEM((CHAINS, width, rows), bf16),
            dma((pairs + 2 * steps,)),
            dma((pairs + steps,)),
            dma((pairs + steps,)),
            dma((2, CHAINS, 2)),
            dma((2, CHAINS, 2)),
            dma((2, CHAINS, 2, PIECES)),
            dma((2, CHAINS, 2, PIECES)),
            dma((steps, 2)),
            dma((steps, 2)),
            dma((steps, 2)),
            dma((3, 2)),
            pltpu.SemaphoreType.REGULAR((3,)),
        ],
        compiler_params=pltpu.CompilerParams(
            collective_id=0, has_side_effects=True, vmem_limit_bytes=67043328
        ),
    )(factor_blocks, inverse_blocks, right_sides)
    return solved.transpose(0, 2, 1)


def plain_solve(factor_blocks, inverse_blocks, right_sides):
    steps_total = right_sides.shape[0]
    solved = []
    outputs = []
    for block_row in range(steps_total):
        residual = right_sides[block_row].astype(jnp.float32)
        if block_row > 0:
            partial_value = jnp.zeros(residual.shape, jnp.float32)
            for column_index in range(block_row):
                partial_value = partial_value + jnp.dot(
                    factor_blocks[pair_index(block_row, column_index)],
                    solved[column_index],
                    preferred_element_type=jnp.float32,
                )
            residual = residual - lax.psum(partial_value, "col")
        residual_bf = residual.astype(jnp.bfloat16)
        term = jnp.dot(inverse_blocks[block_row], residual_bf, preferred_element_type=jnp.float32)
        share = lax.psum_scatter(term, "row", scatter_dimension=1, tiled=True).astype(jnp.bfloat16)
        outputs.append(share)
        if block_row + 1 < steps_total:
            solved.append(lax.all_gather(share, "row", axis=1, tiled=True))
    return jnp.stack(outputs, axis=0)


def solution(mesh):
    placed = (P("groups", "row", "col"), P("groups", "col", "row"), P("groups", "row", None))
    per_device = line_solve if mesh.shape["row"] == 4 and mesh.shape["col"] == 4 else plain_solve
    return jax.shard_map(
        per_device, mesh=mesh, in_specs=placed, out_specs=P("groups", "col", "row"), check_vma=False
    )
```

```python
import jax
import jax.numpy as jnp
from jax import lax
from jax.experimental import pallas as pl
from jax.experimental.pallas import tpu as pltpu
from jax.sharding import PartitionSpec as P

MESH = pl.DeviceIdType.MESH
CHAINS = 2
PIECES = 4
INVERSE_SLOTS = 3
MORE = 6
f32, bf16 = jnp.float32, jnp.bfloat16


def pair_index(block_row, column_index):
    return block_row * (block_row - 1) // 2 + column_index


def dot_t(a, b):
    return lax.dot_general(a, b, (((1,), (1,)), ((), ())), preferred_element_type=f32)


def kernel(
    factor_hbm, inverse_hbm, right_hbm, solved,
    factor, inverse, right, turned, x, in_right, in_left, out, term, partial, ahead, far_out, far_in, residual,
    load_sem, push_send, push_recv, far_send, far_recv, line_send, line_recv, give_send, give_recv, keep_sem, first_sem, credit,
):
    steps, width = solved.shape[:2]
    piece = x.shape[4]
    pairs = factor_hbm.shape[0]
    rows = right.shape[1]
    factor_slots = factor.shape[0]
    row = lax.axis_index("row")
    col = lax.axis_index("col")
    group = lax.axis_index("groups")
    core = lax.rem(col, 2)
    side = col // 2
    sibling = (group, row, col + 1 - 2 * core)
    far = (group, row, lax.rem(col + 2, 4))
    left = (group, jnp.maximum(row - 1, 0), col)
    right_dev = (group, jnp.minimum(row + 1, 3), col)
    last = steps - 1

    def remote(src, dst, send, recv, peer):
        return pltpu.make_async_remote_copy(
            src_ref=src, dst_ref=dst, send_sem=send, recv_sem=recv, device_id=peer, device_id_type=MESH
        )

    def span(p):
        return pl.ds(pl.multiple_of(lax.rem(p, 2) * piece, piece), piece)

    def local_tile(kind, at):
        if kind == "f":
            return pltpu.make_async_copy(factor_hbm.at[at], factor.at[at % factor_slots, core], load_sem.at[at])
        return pltpu.make_async_copy(inverse_hbm.at[at], inverse.at[at % INVERSE_SLOTS, core], load_sem.at[pairs + at])

    def pushed_tile(kind, at):
        if kind == "f":
            dst = factor.at[at % factor_slots, core]
            return remote(factor_hbm.at[at], dst, push_send.at[0], push_recv.at[at], sibling)
        dst = inverse.at[at % INVERSE_SLOTS, core]
        return remote(inverse_hbm.at[at], dst, push_send.at[1], push_recv.at[pairs + at], sibling)

    def landed_tile(kind, at):
        if kind == "f":
            dst = factor.at[at % factor_slots, 1 - core]
            return remote(factor_hbm.at[at], dst, push_send.at[0], push_recv.at[at], sibling)
        dst = inverse.at[at % INVERSE_SLOTS, 1 - core]
        return remote(inverse_hbm.at[at], dst, push_send.at[1], push_recv.at[pairs + at], sibling)

    tiles = [("i", 0)]
    for i in range(1, steps):
        tiles += [("f", pair_index(i, j)) for j in range(i)] + [("i", i)]
    fresh = [t for t in tiles if not (t[0] == "f" and t[1] >= factor_slots or t[0] == "i" and t[1] >= INVERSE_SLOTS)]
    early = [t for t in fresh if t[0] == "i" or t[1] < pair_index(4, 0)]
    late = [t for t in fresh if t not in early]
    ready = {tiles[0]}

    def loaded(kind, at):
        if (kind, at) not in ready:
            ready.add((kind, at))
            local_tile(kind, at).wait()
            landed_tile(kind, at).wait_recv()

    lanes = pl.ds(pl.multiple_of(core * CHAINS * width, CHAINS * width), CHAINS * width)

    def right_load(i):
        return pltpu.make_async_copy(right_hbm.at[i, :, lanes], right.at[i], load_sem.at[pairs + steps + i])

    def first_load(h):
        return pltpu.make_async_copy(inverse_hbm.at[0, span(h)], inverse.at[0, core, span(h)], first_sem.at[0, h])

    def first_push(h, par):
        return remote(inverse_hbm.at[0, span(h)], inverse.at[0, par, span(h)], first_sem.at[1, h], first_sem.at[2, h], sibling)

    right_load(0).start()
    for h in range(2):
        first_load(h).start()
    for i in range(1, steps):
        right_load(i).start()
    for kind, at in fresh[1:]:
        local_tile(kind, at).start()

    barrier = pltpu.get_barrier_semaphore()
    for peer in (sibling, far):
        pl.semaphore_signal(barrier, inc=1, device_id=peer, device_id_type=MESH)

    @pl.when(row > 0)
    def _():
        pl.semaphore_signal(barrier, inc=1, device_id=left, device_id_type=MESH)

    @pl.when(row < 3)
    def _():
        pl.semaphore_signal(barrier, inc=1, device_id=right_dev, device_id_type=MESH)

    @pl.when(jnp.logical_or(row == 0, row == 3))
    def _():
        pl.semaphore_wait(barrier, 3)

    @pl.when(jnp.logical_and(row > 0, row < 3))
    def _():
        pl.semaphore_wait(barrier, 4)

    for h in range(2):
        first_push(h, core).start()
    for kind, at in early[1:]:
        pushed_tile(kind, at).start()

    def turn(i):
        right_load(i).wait()
        turned[i] = right[i].T

    def going_right(i, k, p, src, dst):
        return remote(src, dst, line_send.at[i % 2, k, 0], line_recv.at[i % 2, k, 0, p], right_dev)

    def going_left(i, k, p, src, dst):
        return remote(src, dst, line_send.at[i % 2, k, 1], line_recv.at[i % 2, k, 1, p], left)

    def each(body, start=0, turned_by=0):
        def step(p, carry):
            p = lax.rem(p + turned_by, PIECES)
            body(p, 2 * side + p // 2)
            return carry

        lax.fori_loop(start, PIECES, step, 0)

    def order(i):
        if i == 0:
            return 2 * core
        return 2 * (1 - core) if i == last else 0

    def solve(i, k):
        chain = slice(k * width, (k + 1) * width)
        if i == 0:
            residual[k] = turned[0, chain, :]
        else:
            for h in range(2):
                cols = slice(h * (rows // 2), (h + 1) * (rows // 2))
                far_copy(i, k, h).wait_recv()
                total = partial[k, :, cols] + far_in[i - 1, k, h].astype(f32)
                residual[k, :, cols] = (turned[i, chain, cols].astype(f32) - total).astype(bf16)
        loaded("i", i)
        par = i % 2
        goal = 2 * core + k
        if i >= 2:
            sent(i - 2, k)

        def body(p, c):
            if i == 0 and k == 0:
                @pl.when(p // 2 == core)
                def _():
                    first_load(lax.rem(p, 2)).wait()

                @pl.when(p // 2 != core)
                def _():
                    first_push(lax.rem(p, 2), 1 - core).wait_recv()

            @pl.when(c >= row)
            def _():
                value = dot_t(residual[k], inverse[i % INVERSE_SLOTS, p // 2, span(p), :])
                term[k, p] = value
                out[par, k, p] = value.astype(bf16)
                if i < last:
                    @pl.when(jnp.logical_and(row == 0, c == 0))
                    def _():
                        x[i, k, p] = value.astype(bf16)
                        going_right(i, k, p, x.at[i, k, p], x.at[i, k, p]).start()

                    @pl.when(jnp.logical_and(row == 0, c > 0))
                    def _():
                        going_right(i, k, p, out.at[par, k, p], in_right.at[par, k, p]).start()

                    @pl.when(jnp.logical_and(row >= 2, c == row))
                    def _():
                        going_left(i, k, p, out.at[par, k, p], in_left.at[par, k, p]).start()
                else:
                    @pl.when(jnp.logical_and(row == 0, goal > 0))
                    def _():
                        going_right(i, k, p, out.at[par, k, p], in_right.at[par, k, p]).start()

                    @pl.when(jnp.logical_and(row > goal, c == row))
                    def _():
                        going_left(i, k, p, out.at[par, k, p], in_left.at[par, k, p]).start()

        each(body, 0, order(i))

    def came_right(i, k, p):
        going_right(i, k, p, out.at[0, k, p], in_right.at[0, k, p]).wait_recv()

    def came_left(i, k, p):
        going_left(i, k, p, out.at[0, k, p], in_left.at[0, k, p]).wait_recv()

    def relay_first(i, k, p, c):
        par = i % 2

        @pl.when(row == 1)
        def _():
            came_right(i, k, p)

            @pl.when(c == 0)
            def _():
                going_right(i, k, p, x.at[i, k, p], x.at[i, k, p]).start()

            @pl.when(c == 1)
            def _():
                x[i, k, p] = (in_right[par, k, p].astype(f32) + term[k, p]).astype(bf16)
                going_right(i, k, p, x.at[i, k, p], x.at[i, k, p]).start()
                going_left(i, k, p, x.at[i, k, p], x.at[i, k, p]).start()

            @pl.when(c >= 2)
            def _():
                out[par, k, p] = (in_right[par, k, p].astype(f32) + term[k, p]).astype(bf16)
                going_right(i, k, p, out.at[par, k, p], in_right.at[par, k, p]).start()

        @pl.when(jnp.logical_and(row == 2, c == 3))
        def _():
            came_left(i, k, p)
            out[par, k, p] = (in_left[par, k, p].astype(f32) + term[k, p]).astype(bf16)
            going_left(i, k, p, out.at[par, k, p], in_left.at[par, k, p]).start()

    def relay_second(i, k, p, c):
        par = i % 2

        @pl.when(jnp.logical_and(row == 1, c >= 2))
        def _():
            came_left(i, k, p)
            x[i, k, p] = (out[par, k, p].astype(f32) + in_left[par, k, p].astype(f32)).astype(bf16)
            going_left(i, k, p, x.at[i, k, p], x.at[i, k, p]).start()

        @pl.when(row == 2)
        def _():
            came_right(i, k, p)

            @pl.when(c >= 2)
            def _():
                x[i, k, p] = (out[par, k, p].astype(f32) + in_right[par, k, p].astype(f32)).astype(bf16)

            going_right(i, k, p, x.at[i, k, p], x.at[i, k, p]).start()

    def came_last(i, k, p, c):
        @pl.when(jnp.logical_and(row == 0, c >= 1))
        def _():
            came_left(i, k, p)

        @pl.when(row == 3)
        def _():
            came_right(i, k, p)

    def sent(i, k):
        goal = 2 * core + k
        to_right = row < 3 if i < last else row < goal
        to_left = row > 0 if i < last else row > goal
        most = 2 * side >= row

        def wait(way, pieces):
            ref = out.at[0, k, pl.ds(0, pieces)]
            remote(ref, ref, line_send.at[i % 2, k, way], line_recv.at[0, k, way, 0], sibling).wait_send()

        @pl.when(to_right)
        def _():
            wait(0, PIECES)

        @pl.when(jnp.logical_and(to_left, most))
        def _():
            wait(1, PIECES)

        @pl.when(jnp.logical_and(to_left, jnp.logical_and(jnp.logical_not(most), 2 * side + 1 >= row)))
        def _():
            wait(1, PIECES // 2)

    def collect(i, k):
        par = i % 2
        goal = 2 * core + k

        @pl.when(jnp.logical_and(row < goal, row >= 1))
        def _():
            def body(p, c):
                came_right(i, k, p)

                @pl.when(c >= row)
                def _():
                    out[par, k, p] = (in_right[par, k, p].astype(f32) + term[k, p]).astype(bf16)
                    going_right(i, k, p, out.at[par, k, p], in_right.at[par, k, p]).start()

                @pl.when(c < row)
                def _():
                    going_right(i, k, p, in_right.at[par, k, p], in_right.at[par, k, p]).start()

            each(body, 0, order(i))

        @pl.when(row > goal)
        def _():
            def body(p, c):
                @pl.when(c > row)
                def _():
                    came_left(i, k, p)
                    out[par, k, p] = (in_left[par, k, p].astype(f32) + term[k, p]).astype(bf16)
                    going_left(i, k, p, out.at[par, k, p], in_left.at[par, k, p]).start()

            each(body, 0, order(i))

    def keep(i, k):
        par = i % 2
        goal = 2 * core + k

        @pl.when(row == goal)
        def _():
            def body(p, c):
                @pl.when(row >= 1)
                def _():
                    came_right(i, k, p)

                @pl.when(c > row)
                def _():
                    came_left(i, k, p)

                @pl.when(c < row)
                def _():
                    x[i, k, p] = in_right[par, k, p]

                @pl.when(c >= row)
                def _():
                    @pl.when(row >= 1)
                    def _():
                        term[k, p] = term[k, p] + in_right[par, k, p].astype(f32)

                    @pl.when(c > row)
                    def _():
                        term[k, p] = term[k, p] + in_left[par, k, p].astype(f32)

                    x[i, k, p] = term[k, p].astype(bf16)

                @pl.when(p // 2 == core)
                def _():
                    keep_copy(i, lax.rem(p, 2)).start()

                @pl.when(p // 2 != core)
                def _():
                    give_copy(i, lax.rem(p, 2)).start()

            each(body, 0, order(i))

    def far_copy(i, k, h):
        return remote(far_out.at[i - 1, k, h], far_in.at[i - 1, k, h], far_send.at[i % 2, k, h], far_recv.at[i % 2, k, h], far)

    def update(i, k):
        at = pair_index(i, i - 1)
        loaded("f", at)
        if i > 1:
            partial[k] = ahead[i - 2, k * width : (k + 1) * width, :]
        else:
            partial[k] = jnp.zeros_like(partial[k])

        def body(p, c):
            came_last(i - 1, k, p, c)
            partial[k] += dot_t(x[i - 1, k, p], factor[at % factor_slots, p // 2, :, span(p)])

        each(body, 0, order(i - 1))
        for h in range(2):
            if i > 2:
                far_copy(i - 2, k, h).wait_send()
            far_out[i - 1, k, h] = partial[k, :, h * (rows // 2) : (h + 1) * (rows // 2)].astype(bf16)
            far_copy(i, k, h).start()

    begun = set()

    def look_ahead(i, j, par, h):
        at = pair_index(i, j)
        loaded("f", at)
        known = [x[j, :, 2 * par + q].reshape(CHAINS * width, piece) for q in range(2)]
        cols = slice(h * piece, (h + 1) * piece)
        value = dot_t(jnp.concatenate(known, axis=1), factor[at % factor_slots, par, cols, :])
        if (i, h) in begun:
            value = value + ahead[i - 2, :, cols]
        begun.add((i, h))
        ahead[i - 2, :, cols] = value

    waiting = [(i, j, par, h) for i in range(2, steps) for j in range(i - 1) for par in range(2) for h in range(2)]

    def take(units):
        for unit in units:
            waiting.remove(unit)
        return units

    def look_due(i):
        return take([u for u in waiting if u[0] == i + 1])

    def look_more(i):
        return take([u for u in waiting if u[0] > i + 1 and u[1] < i][:MORE])

    def relay(i, k, units):
        units = list(units)
        for stage in (relay_first, relay_second):
            for q in range(PIECES):
                p = lax.rem(q + order(i), PIECES)
                stage(i, k, p, 2 * side + p // 2)
                if units:
                    look_ahead(*units.pop(0))
        for unit in units:
            look_ahead(*unit)

    owner = core == row // 2
    chain_at = lax.rem(row, 2)

    def give_copy(i, h):
        p = 2 * (1 - core) + h
        return remote(x.at[i, chain_at, p], solved.at[i, :, span(h)], give_send.at[i // last], give_recv.at[i // last], sibling)

    def keep_copy(i, h):
        return pltpu.make_async_copy(x.at[i, chain_at, 2 * core + h], solved.at[i, :, span(h)], keep_sem.at[i // last])

    def give(i):
        @pl.when(owner)
        def _():
            for h in range(2):
                give_copy(i, h).start()
                keep_copy(i, h).start()

    def allow(n):
        pl.semaphore_signal(credit.at[n], inc=1, device_id=sibling, device_id_type=MESH)

    def refill(n, kind, at):
        pl.semaphore_wait(credit.at[n], 1)
        local_tile(kind, at).start()
        pushed_tile(kind, at).start()

    def settle_gives(n):
        ref = x.at[pl.ds(n * last, 1 if n else last), 0, pl.ds(0, 2)]
        gift = remote(ref, ref, give_send.at[n], give_recv.at[n], sibling)

        @pl.when(owner)
        def _():
            gift.wait_send()
            pltpu.make_async_copy(ref, ref, keep_sem.at[n]).wait()

        @pl.when(jnp.logical_not(owner))
        def _():
            gift.wait_recv()

    def settle():
        settle_gives(0)
        for k in range(CHAINS):
            sent(last - 1, k)
        for i in range(steps - 2, steps):
            for k in range(CHAINS):
                for h in range(2):
                    far_copy(i, k, h).wait_send()
        for h in range(2):
            first_push(h, core).wait_send()
        for kind, ref in enumerate((factor_hbm, inverse_hbm.at[pl.ds(1, steps - 1)])):
            remote(ref, ref, push_send.at[kind], push_recv.at[kind], sibling).wait_send()

    a, b = 0, 1
    turn(0)
    solve(0, a)
    solve(0, b)
    allow(0)
    turn(1)
    relay(0, a, [])
    update(1, a)
    refill(0, "i", 3)
    for kind, at in late:
        pushed_tile(kind, at).start()
    relay(0, b, [])
    for i in range(1, steps):
        solve(i, a)
        update(i, b)
        give(i - 1)
        if i == 1:
            allow(1)
        if i < last:
            relay(i, a, look_due(i))
            solve(i, b)
            if i == 1:
                allow(2)
            turn(i + 1)
            update(i + 1, a)
            if i == 1:
                refill(1, "f", factor_slots)
                refill(2, "i", 4)
            relay(i, b, look_more(i))
        else:
            collect(i, a)
            solve(i, b)
            collect(i, b)
            settle()
            keep(i, a)
            keep(i, b)

    settle_gives(1)
    for k in range(CHAINS):
        sent(last, k)


def line_solve(factor_blocks, inverse_blocks, right_sides):
    steps, rows, angles = right_sides.shape
    pairs = factor_blocks.shape[0]
    col_rows = inverse_blocks.shape[1]
    width = angles // lax.axis_size("row")
    both = CHAINS * width
    half = rows // 2
    piece = col_rows // 2
    line = (2, CHAINS, PIECES, width, piece)
    dma = pltpu.SemaphoreType.DMA
    solved = pl.pallas_call(
        kernel,
        out_shape=jax.ShapeDtypeStruct((steps, width, col_rows), bf16),
        in_specs=[pl.BlockSpec(memory_space=pl.ANY)] * 3,
        out_specs=pl.BlockSpec(memory_space=pl.ANY),
        scratch_shapes=[
            pltpu.VMEM((pairs - 1, 2) + factor_blocks.shape[1:], bf16),
            pltpu.VMEM((INVERSE_SLOTS, 2) + inverse_blocks.shape[1:], bf16),
            pltpu.VMEM((steps, rows, both), bf16),
            pltpu.VMEM((steps, both, rows), bf16),
            pltpu.VMEM((steps, CHAINS, PIECES, width, piece), bf16),
            pltpu.VMEM(line, bf16),
            pltpu.VMEM(line, bf16),
            pltpu.VMEM(line, bf16),
            pltpu.VMEM((CHAINS, PIECES, width, piece), f32),
            pltpu.VMEM((CHAINS, width, rows), f32),
            pltpu.VMEM((steps - 2, both, rows), f32),
            pltpu.VMEM((steps - 1, CHAINS, 2, width, half), bf16),
            pltpu.VMEM((steps - 1, CHAINS, 2, width, half), bf16),
            pltpu.VMEM((CHAINS, width, rows), bf16),
            dma((pairs + 2 * steps,)),
            dma((2,)),
            dma((pairs + steps,)),
            dma((2, CHAINS, 2)),
            dma((2, CHAINS, 2)),
            dma((2, CHAINS, 2)),
            dma((2, CHAINS, 2, PIECES)),
            dma((2,)),
            dma((2,)),
            dma((2,)),
            dma((3, 2)),
            pltpu.SemaphoreType.REGULAR((3,)),
        ],
        compiler_params=pltpu.CompilerParams(
            collective_id=0, has_side_effects=True, vmem_limit_bytes=67043328
        ),
    )(factor_blocks, inverse_blocks, right_sides)
    return solved.transpose(0, 2, 1)


def plain_solve(factor_blocks, inverse_blocks, right_sides):
    steps_total = right_sides.shape[0]
    solved = []
    outputs = []
    for block_row in range(steps_total):
        residual = right_sides[block_row].astype(jnp.float32)
        if block_row > 0:
            partial_value = jnp.zeros(residual.shape, jnp.float32)
            for column_index in range(block_row):
                partial_value = partial_value + jnp.dot(
                    factor_blocks[pair_index(block_row, column_index)],
                    solved[column_index],
                    preferred_element_type=jnp.float32,
                )
            residual = residual - lax.psum(partial_value, "col")
        residual_bf = residual.astype(jnp.bfloat16)
        term = jnp.dot(inverse_blocks[block_row], residual_bf, preferred_element_type=jnp.float32)
        share = lax.psum_scatter(term, "row", scatter_dimension=1, tiled=True).astype(jnp.bfloat16)
        outputs.append(share)
        if block_row + 1 < steps_total:
            solved.append(lax.all_gather(share, "row", axis=1, tiled=True))
    return jnp.stack(outputs, axis=0)


def solution(mesh):
    placed = (P("groups", "row", "col"), P("groups", "col", "row"), P("groups", "row", None))
    per_device = line_solve if mesh.shape["row"] == 4 and mesh.shape["col"] == 4 else plain_solve
    return jax.shard_map(
        per_device, mesh=mesh, in_specs=placed, out_specs=P("groups", "col", "row"), check_vma=False
    )
```
